128 devices in a mesh: dp: 4 (over z_hi, core), ctx: 32 (over y, z_lo, x).
Axes of the slice: x: 4, y: 4, z: 4 (z_hi: 2, z_lo: 2; z = z_hi * 2 + z_lo), core: 2. Of those that a mesh axis runs over, the one named last changes fastest.
Arguments:
- feats: bfloat16 [4, 3, 4096, 4096], P('dp', None, 'ctx'), may hold values from -6 to 6
- grad_y: bfloat16 [4, 4096, 4096], P('dp', 'ctx'), may hold values from -6 to 6
- short_w: float32 [7, 3, 4096], replicated, may hold values from -2 to 2
- long_h: float32 [4096, 4096], P(None, 'ctx'), may hold values from -2 to 2
- block_order: int32 [64], replicated, may hold values from 0 to 63, as said below
Outputs:
- mixed: bfloat16 [4, 4096, 4096], P('dp', 'ctx')
- feats_grad: bfloat16 [4, 3, 4096, 4096], P('dp', None, 'ctx')
- short_grad: float32 [7, 3, 4096], P(None, None, 'ctx')
- filter_grad: float32 [4096, 4096], P(None, 'ctx')
The draws below stay inside these ranges and needn't reach their ends.
Inputs may be any that keep to these rules, and one draw needn't show every extreme that they name: Stored blocks 2 i and 2 i + 1 (those of index i of ctx) hold sequence blocks i and 63 - i, in an order drawn for each i; block_order is a permutation.
All inputs are finite; a program needn't handle non-finite values.
Results may differ from the reference program's by a relative error of at most 0.0085.
Values may be sent and summed in bfloat16 or wider, within the bound.
A program may use at most 192 MiB of HBM per device.

```python
import jax
import jax.numpy as jnp

D = 4096
KERNEL = 7
SEQ = 4096
BATCH = 4
BLOCKS = 64


def draw_long_h(key, part):
    key_decay, key_noise = jax.random.split(jax.random.fold_in(key, 11))
    lower_len = 16.0
    upper_len = 2.0 * SEQ
    spread = jax.random.uniform(key_decay, (1, D), jnp.float32)
    decay_len = jnp.exp(jnp.log(lower_len) + spread * (jnp.log(upper_len) - jnp.log(lower_len)))
    positions = jnp.arange(SEQ, dtype=jnp.float32)[:, None]
    amplitude = 1.0 / jnp.sqrt(jnp.minimum(decay_len, float(SEQ)))
    envelope = amplitude * jnp.exp(-positions / decay_len)
    noise_part = jnp.clip(jax.random.normal(key_noise, (SEQ, D), jnp.float32), -5.0, 5.0)
    values = envelope * noise_part
    return values.astype(jnp.float32)


def draw_block_order(key, part):
    half_count = BLOCKS // 2
    flips = jax.random.randint(jax.random.fold_in(key, 23), (half_count,), 0, 2)
    device_ids = jnp.arange(half_count, dtype=jnp.int32)
    low_ids = device_ids
    high_ids = BLOCKS - 1 - device_ids
    first_ids = jnp.where(flips == 1, high_ids, low_ids)
    second_ids = jnp.where(flips == 1, low_ids, high_ids)
    return jnp.stack([first_ids, second_ids], 1).reshape(BLOCKS).astype(jnp.int32)


def shard_levels(rng, dims, shards, low, top_value):
    def one(position, parts):
        draws = jax.random.uniform(jax.random.fold_in(jax.random.fold_in(rng, 6), position), (parts,), jnp.float32, low / len(shards), top_value / len(shards))
        return jnp.repeat(jnp.exp(draws), dims[position] // parts).reshape((-1,) + (1,) * (len(dims) - position - 1))

    level = one(*shards[0])
    for cut in shards[1:]:
        level = level * one(*cut)
    return level


def noise(own_key, shape, scale, reach, cuts=(), held_as=jnp.bfloat16):
    array = scale * jax.random.normal(own_key, shape, jnp.float32)
    if cuts:
        array = array * shard_levels(own_key, shape, cuts, -0.22, 0.18)
    return jnp.clip(array, -reach, reach).astype(held_as)


def setup_inputs(seed: int = 0) -> dict:
    key_list = jax.random.split(jax.random.key(seed), 6)
    feats = noise(key_list[0], (BATCH, 3, SEQ, D), 1.0, 6.0, ((0, 4), (2, 32)))
    grad_y = noise(key_list[1], (BATCH, SEQ, D), 1.0, 6.0, ((0, 4), (1, 32)))
    short_w = noise(key_list[2], (KERNEL, 3, D), KERNEL ** -0.5, 2.0, (), jnp.float32)
    long_h = draw_long_h(jax.random.fold_in(key_list[5], 71), 0)
    block_order = draw_block_order(jax.random.fold_in(key_list[5], 71), 0)
    return dict(feats=feats, grad_y=grad_y, short_w=short_w, long_h=long_h, block_order=block_order)


def reorder(values, table, block_count, axis):
    shape_full = values.shape
    row_total = shape_full[axis]
    grouped = values.reshape(shape_full[:axis] + (block_count, row_total // block_count) + shape_full[axis + 1:])
    return jnp.take(grouped, table, axis=axis).reshape(shape_full)


def featurize(padded, weights, rows):
    tap_count = weights.shape[0]
    total = jnp.zeros((padded.shape[0], rows, padded.shape[2]), jnp.float32)
    for offset in range(tap_count):
        begin = tap_count - 1 - offset
        total = total + weights[offset] * padded[:, begin:begin + rows].astype(jnp.float32)
    return total


def spread_back(extended, weights, rows):
    tap_count = weights.shape[0]
    total = jnp.zeros((extended.shape[0], rows, extended.shape[2]), jnp.float32)
    for offset in range(tap_count):
        total = total + weights[offset] * extended[:, offset:offset + rows]
    return total


def weight_terms(grads, padded, rows):
    tap_count = KERNEL
    terms = []
    for offset in range(tap_count):
        begin = tap_count - 1 - offset
        terms.append(jnp.sum(grads * padded[:, begin:begin + rows].astype(jnp.float32), axis=1))
    return jnp.stack(terms, 0)


def reference(feats, grad_y, short_w, long_h, block_order):
    block_count = BLOCKS
    numbers = jnp.arange(block_count, dtype=jnp.int32)
    source = jnp.sum(numbers[None, :] * (block_order[None, :] == numbers[:, None]).astype(jnp.int32), axis=1).astype(jnp.int32)
    rim_rows = KERNEL - 1
    length_full = 2 * SEQ
    tap_w = short_w[:, :, None, :]
    filter_spec = jnp.fft.rfft(long_h, n=length_full, axis=0)
    mixed_list = []
    grad_list = []
    short_total = jnp.zeros((KERNEL, 3, D), jnp.float32)
    filter_total = jnp.zeros((SEQ, D), jnp.float32)
    for seq_index in range(BATCH):
        raw_seq = reorder(feats[seq_index], source, block_count, 1)
        padded_x = jnp.concatenate([jnp.zeros((3, rim_rows, D), jnp.bfloat16), raw_seq], 1)
        featured = featurize(padded_x, tap_w, SEQ).astype(jnp.bfloat16)
        query_f = featured[0].astype(jnp.float32)
        key_part = featured[1].astype(jnp.float32)
        value_part = featured[2].astype(jnp.float32)
        gated = (key_part * value_part).astype(jnp.bfloat16)
        gated_spec = jnp.fft.rfft(gated.astype(jnp.float32), n=length_full, axis=0)
        conv_out = jnp.fft.irfft(gated_spec * filter_spec, n=length_full, axis=0)[:SEQ]
        mixed_seq = (query_f * conv_out).astype(jnp.bfloat16)
        grad_seq = reorder(grad_y[seq_index], source, block_count, 0).astype(jnp.float32)
        grad_query = (grad_seq * conv_out).astype(jnp.bfloat16)
        grad_conv = grad_seq * query_f
        back_spec = jnp.fft.rfft(grad_conv, n=length_full, axis=0)
        grad_gated = jnp.fft.irfft(back_spec * jnp.conj(filter_spec), n=length_full, axis=0)[:SEQ].astype(jnp.bfloat16)
        filter_part = jnp.fft.irfft(back_spec * jnp.conj(gated_spec), n=length_full, axis=0)[:SEQ]
        gate_grad = grad_gated.astype(jnp.float32)
        grad_feat = jnp.stack([grad_query.astype(jnp.float32), gate_grad * value_part, gate_grad * key_part], 0)
        extended = jnp.concatenate([grad_feat, jnp.zeros((3, rim_rows, D), jnp.float32)], 1)
        grad_x = spread_back(extended, tap_w, SEQ).astype(jnp.bfloat16)
        short_total = short_total + weight_terms(grad_feat, padded_x, SEQ)
        filter_total = filter_total + filter_part.astype(jnp.float32)
        mixed_list.append(reorder(mixed_seq, block_order, block_count, 0))
        grad_list.append(reorder(grad_x, block_order, block_count, 1))
    return jnp.stack(mixed_list, 0), jnp.stack(grad_list, 0), short_total, filter_total
```

```python
import jax
import jax.numpy as jnp
import numpy as np
from jax import lax
from jax.experimental import pallas as pl
from jax.experimental.pallas import tpu as pltpu
from jax.sharding import PartitionSpec as P

MESH = pl.DeviceIdType.MESH
F32 = jnp.float32
BF16 = jnp.bfloat16
LANES = 128
TAPS = 7
ROWS = 64
WIDE = 72
OUTER = 32
GROUPS = 16
ORDER = tuple(range(OUTER // 2)) + tuple(range(OUTER - 1, OUTER // 2 - 1, -1))


def dft_tables():
    k1 = np.arange(OUTER)[:, None, None, None] + 0.5
    r = np.array(ORDER)[None, None, :, None]
    n_out = np.arange(8)[None, :, None, None]
    n_in = np.arange(8)[None, None, None, :]
    angle = 2.0 * np.pi * (r * k1 / 64.0 + n_in * k1 / 8192.0)
    keep = (n_out == n_in).astype(np.float64)
    outer = np.stack([np.cos(angle) * keep, -np.sin(angle) * keep], 1).reshape(OUTER * 16, OUTER * 8)
    n2 = np.arange(LANES)
    turn = 2.0 * np.pi * ((n2[:, None] * n2[None, :]) % LANES) / LANES
    inner = np.block([[np.cos(turn), np.sin(turn)], [-np.sin(turn), np.cos(turn)]])
    group = 2.0 * np.pi * np.arange(GROUPS)[:, None] * 8.0 * (np.arange(OUTER)[None, :] + 0.5) / 8192.0
    half = lambda a: np.asarray(np.asarray(a, np.float32), BF16)
    flat = lambda a: np.asarray(a, np.float32).reshape(-1)
    return (half(outer), half(outer.T / 4096.0), half(inner), half(inner.T), flat(np.cos(group)), flat(np.sin(group)))


def turn(i):
    a, b, c = i % 4, i // 4 % 4, i // 16
    return 8 * ((10 - a - b) % 4) + 4 * ((a + b + c + 1) % 2) + (6 - a) % 4


STEPS = [turn(i) for i in range(32) if turn(i)]


def ctx_peer(me, k):
    y, z, x = me // 8 + k // 8, me // 4 + k // 4, me + k
    return (lax.rem(y, 4) * 2 + lax.rem(z, 2)) * 4 + lax.rem(x, 4)


def ctx_source(me, k):
    y, z, x = me // 8 + 4 - k // 8, me // 4 + k // 4, me + 4 - lax.rem(k, 4)
    return (lax.rem(y, 4) * 2 + lax.rem(z, 2)) * 4 + lax.rem(x, 4)


def remote(src, dst, ssem, rsem, device):
    return pltpu.make_async_remote_copy(
        src_ref=src, dst_ref=dst, send_sem=ssem, recv_sem=rsem, device_id=device, device_id_type=MESH
    )


def wide_rows(h):
    return pl.ds(pl.multiple_of(h * 16, 16), 16)


def place(p):
    return (p, 0) if p < OUTER else (2 * OUTER - 1 - p, 1)


def scalars(cos_ref, sin_ref, h, k):
    first, second = 2 * h * OUTER + k, (2 * h + 1) * OUTER + k
    return cos_ref[first], sin_ref[first], cos_ref[second], sin_ref[second]


def outer_step(cos_ref, sin_ref, outer, pieces, mid, h):
    data = jnp.concatenate(
        [jnp.concatenate([v[:8] for v in pieces], 0), jnp.concatenate([v[8:] for v in pieces], 0)], 1
    ).astype(BF16)
    out = jnp.dot(outer[...], data, preferred_element_type=F32)
    for k in range(OUTER):
        c0, s0, c1, s1 = scalars(cos_ref, sin_ref, h, k)
        re, im = out[16 * k : 16 * k + 8], out[16 * k + 8 : 16 * k + 16]
        re0, re1, im0, im1 = re[:, :LANES], re[:, LANES:], im[:, :LANES], im[:, LANES:]
        mid[2 * k, wide_rows(h), :] = jnp.concatenate([re0 * c0 + im0 * s0, re1 * c1 + im1 * s1], 0).astype(BF16)
        mid[2 * k + 1, wide_rows(h), :] = jnp.concatenate([im0 * c0 - re0 * s0, im1 * c1 - re1 * s1], 0).astype(BF16)


def inner_forward(inner, mid, m):
    rows = [mid[pl.ds(4 * m + 2 * i, 2)].reshape(2 * LANES, LANES) for i in range(2)]
    return jnp.dot(inner[...], jnp.concatenate(rows, 1), preferred_element_type=F32)


def inner_inverse(cos_ref, sin_ref, inner_t, re, im, m, turned):
    prod = jnp.concatenate([re.astype(BF16), im.astype(BF16)], 0)
    back = jnp.dot(inner_t[...], prod, preferred_element_type=F32)
    for i in range(2):
        lanes = slice(i * LANES, (i + 1) * LANES)
        k = 2 * m + i
        for h in range(GROUPS // 2):
            c0, s0, c1, s1 = scalars(cos_ref, sin_ref, h, k)
            re0, re1 = back[16 * h : 16 * h + 8, lanes], back[16 * h + 8 : 16 * h + 16, lanes]
            im0, im1 = (back[LANES + 16 * h + o : LANES + 16 * h + o + 8, lanes] for o in (0, 8))
            rows = slice(16 * h, 16 * h + 16)
            turned[2 * k, rows, :] = jnp.concatenate([re0 * c0 - im0 * s0, re1 * c1 - im1 * s1], 0).astype(BF16)
            turned[2 * k + 1, rows, :] = jnp.concatenate([im0 * c0 + re0 * s0, im1 * c1 + re1 * s1], 0).astype(BF16)


def outer_inverse(outer_t, turned, h):
    values = turned[:, wide_rows(h), :].astype(F32)
    sides = [values[:, o : o + 8].reshape(OUTER * 16, LANES) for o in (0, 8)]
    out = jnp.dot(outer_t[...], jnp.concatenate(sides, 1).astype(BF16), preferred_element_type=F32)
    pieces = []
    for i in range(OUTER):
        part = out[8 * i : 8 * i + 8]
        pieces.append(jnp.concatenate([part[:, :LANES], part[:, LANES:]], 0))
    return pieces


def both_halves(step):
    for odd in range(2):

        def body(i, carry, odd=odd):
            step(4 * odd + i, odd, wide_rows(i))
            return carry

        lax.fori_loop(0, 4, body, 0, unroll=2)


def hyena_kernel(
    cos_ref, sin_ref, order_ref, outer, outer_t, inner, inner_t, long_h, w_ref, x_hbm, g_hbm,
    mixed_ref, grad_ref, filt, total,
    send, recv, mid, spec_h, spec_g, spec_c, turned, cross, out, local, pair, near, far,
    back, qkv_ref, x_ref, g_ref, shifted, part, held, dp_held,
    tail, head, got_tail, got_head,
    send_in, recv_in, send_out, recv_out, own_sem, dp_send, dp_recv,
    load_sem, part_send, part_recv, sum_send, sum_recv, halo_send, halo_recv,
):
    n = send.shape[1]
    me = lax.axis_index("ctx")
    mine = lax.axis_index("dp")
    core = lax.rem(mine, 2)
    neighbour = {"dp": mine + 1 - 2 * core}
    opposite = {"dp": lax.rem(mine + 2, 4)}
    barrier = pltpu.get_barrier_semaphore()
    for k in STEPS:
        pl.semaphore_signal(barrier, inc=1, device_id={"ctx": ctx_peer(me, k)}, device_id_type=MESH)
    diagonal = {"dp": lax.rem(mine + 3 - 2 * core, 4)}
    for device in (neighbour, opposite, diagonal):
        pl.semaphore_signal(barrier, inc=1, device_id=device, device_id_type=MESH)
    loads = [
        pltpu.make_async_copy(source, target, load_sem.at[i])
        for i, (source, target) in enumerate(((x_hbm, x_ref), (g_hbm, g_ref)))
    ]
    for copy in loads:
        copy.start()
    flip = (order_ref[2 * me] != me).astype(jnp.int32)
    for copy in loads:
        copy.wait()
    for way, (ends, starts) in enumerate(((flip, 1 - flip), (1 - flip, flip))):
        for j in range(3):
            tail[way, j] = x_ref[j, ends, ROWS - 8 :, :]
            head[way, j] = x_ref[j + 1, starts, :8, :] if j < 2 else g_ref[starts, :8, :]
    pl.semaphore_wait(barrier, n + 2)
    aside = ({"ctx": lax.rem(me + 1, n)}, {"ctx": lax.rem(me + n - 1, n)})
    halos = [
        remote(source.at[way], target.at[way], halo_send.at[i, way], halo_recv.at[i, way], aside[way])
        for i, (source, target) in enumerate(((tail, got_tail), (head, got_head)))
        for way in range(2)
    ]
    for copy in halos:
        copy.start()

    def inward(a, k):
        peer = ctx_peer(me, k)
        return remote(send.at[a, peer], recv.at[a, me], send_in.at[a, k], recv_in.at[a, k], {"ctx": peer})

    def outward(a, k):
        peer = ctx_peer(me, k)
        return remote(out.at[a, peer], back.at[a, me], send_out.at[a, k], recv_out.at[a, k], {"ctx": peer})

    def filter_outer(h, odd, row):
        del odd, row
        pieces = [long_h[pl.ds(pl.multiple_of(r * LANES + h * 16, 16), 16), :] for r in ORDER]
        outer_step(cos_ref, sin_ref, outer, pieces, mid, h)

    both_halves(filter_outer)

    def filter_inner(m, carry):
        spec_h[m] = inner_forward(inner, mid, m)
        return carry

    lax.fori_loop(0, OUTER // 2, filter_inner, 0, unroll=2)

    for copy in halos[:2]:
        copy.wait_recv()
    first, last = me == 0, me == n - 1

    def lanes_of(owner):
        return pl.ds(pl.multiple_of(owner * LANES, LANES), LANES)

    def featurize(owner):
        lanes = lanes_of(owner)
        for half in range(2):
            stored = 1 - flip if half else flip
            values = []
            for j in range(3):
                came = got_tail[half, j, :, lanes].astype(F32)
                if half == 0:
                    before = jnp.where(first, jnp.zeros_like(came), came)
                else:
                    before = jnp.where(last, tail[0, j, :, lanes].astype(F32), came)
                shifted[half, j, :8] = before
                shifted[half, j, 8:] = x_ref[j, stored, :, lanes].astype(F32)
                acc = None
                for t in range(TAPS):
                    term = w_ref[j, t : t + 1, lanes] * shifted[half, j, pl.ds(8 - t, ROWS), :]
                    acc = term if acc is None else acc + term
                value = acc.astype(BF16)
                qkv_ref[j, half, :, lanes] = value
                values.append(value.astype(F32))
            send[0, owner, half] = (values[1] * values[2]).astype(BF16)
            send[1, owner, half] = (g_ref[stored, :, lanes].astype(F32) * values[0]).astype(BF16)

    def start_gated(i):
        k = turn(i)

        @pl.when(k > 0)
        def _():
            inward(0, k).start()

    featurize(ctx_peer(me, turn(0)))

    def featurize_next(i, carry):
        featurize(ctx_peer(me, turn(i)))
        start_gated(i - 1)
        return carry

    lax.fori_loop(1, n, featurize_next, 0)
    start_gated(n - 1)
    own_in = [pltpu.make_async_copy(send.at[a, me], recv.at[a, me], own_sem.at[a]) for a in range(2)]
    for copy in own_in:
        copy.start()
    for k in STEPS:
        inward(1, k).start()

    def arrive(a):
        own_in[a].wait()
        for k in STEPS:
            inward(a, k).wait_recv()

        def step(h, odd, row):
            places = [place(2 * r + odd) for r in ORDER]
            pieces = [recv[a, owner, half, row, :].astype(F32) for owner, half in places]
            outer_step(cos_ref, sin_ref, outer, pieces, mid, h)

        both_halves(step)

    def depart(a, turned):
        def step(h, odd, row):
            for r, piece in zip(ORDER, outer_inverse(outer_t, turned, h)):
                owner, half = place(2 * r + odd)
                out[a, owner, half, row, :] = piece.astype(BF16)

        both_halves(step)
        for p in range(2 * n):
            owner, half = place(p)
            if p + 1 < 2 * n:
                after, part = place(p + 1)
                out[a, owner, half, ROWS:, :] = out[a, after, part, : WIDE - ROWS, :]
            else:
                out[a, owner, half, ROWS:, :] = jnp.zeros((WIDE - ROWS, LANES), BF16)
        for k in STEPS:
            outward(a, k).start()
        own = pltpu.make_async_copy(out.at[a, me], back.at[a, me], own_sem.at[2 + a])
        own.start()
        return own

    arrive(0)

    def conv_step(m, carry):
        g = inner_forward(inner, mid, m)
        spec_g[m] = g
        h = spec_h[m]
        gr, gi, hr, hi = g[:LANES], g[LANES:], h[:LANES], h[LANES:]
        inner_inverse(cos_ref, sin_ref, inner_t, gr * hr - gi * hi, gr * hi + gi * hr, m, turned)
        return carry

    lax.fori_loop(0, OUTER // 2, conv_step, 0, unroll=2)
    own_conv = depart(0, turned)

    arrive(1)

    def grad_step(m, carry):
        c = inner_forward(inner, mid, m)
        spec_c[m] = c
        h = spec_h[m]
        cr, ci, hr, hi = c[:LANES], c[LANES:], h[:LANES], h[LANES:]
        inner_inverse(cos_ref, sin_ref, inner_t, cr * hr + ci * hi, ci * hr - cr * hi, m, turned)
        return carry

    lax.fori_loop(0, OUTER // 2, grad_step, 0, unroll=2)

    def cross_step(m, carry):
        c, g = spec_c[m], spec_g[m]
        cr, ci, gr, gi = c[:LANES], c[LANES:], g[:LANES], g[LANES:]
        inner_inverse(cos_ref, sin_ref, inner_t, cr * gr + ci * gi, ci * gr - cr * gi, m, cross)
        return carry

    lax.fori_loop(0, OUTER // 2, cross_step, 0, unroll=2)

    def filter_back(h, odd, row):
        del odd, row
        for r, piece in zip(ORDER, outer_inverse(outer_t, cross, h)):
            local[r, wide_rows(h), :] = piece

    both_halves(filter_back)

    half = OUTER // 2
    kept = pl.ds(core * half, half)
    given = pl.ds((1 - core) * half, half)
    to_pair = remote(local.at[given], pair, dp_send.at[0], dp_recv.at[0], neighbour)
    to_pair.start()
    own_grad = depart(1, turned)

    def add_far(i, carry):
        filt[core * half + i] = near[i].astype(F32) + far[i].astype(F32)
        return carry

    for copy in halos[2:]:
        copy.wait_recv()

    def taps_back(j, half, inside, beyond, source, sums):
        shifted[half, j, :ROWS] = inside
        shifted[half, j, ROWS:] = beyond
        acc = None
        for t in range(TAPS):
            value = shifted[half, j, pl.ds(t, ROWS), :]
            term = w_ref[j, t : t + 1, sums[0]] * value
            acc = term if acc is None else acc + term
            fold = jnp.sum((source * value).reshape(8, 8, LANES), axis=0)
            sums[1][j][t] = fold if half == 0 else sums[1][j][t] + fold
        return acc

    def put_part(owner, j, folds):
        rows = [jnp.sum(value, axis=0, keepdims=True) for value in folds]
        part[owner, 8 * j : 8 * j + 8, :] = jnp.concatenate([*rows, jnp.zeros((1, LANES), F32)], 0)

    def in_order(values):
        keep = flip == 0
        return [jnp.where(keep, values[i], values[1 - i]).astype(BF16) for i in range(2)]

    def after_rows(half, rim, lanes):
        came = got_head[1 - half, rim, :, lanes].astype(F32)
        if half == 0:
            return jnp.where(last, head[0, rim, :, lanes].astype(F32), came)
        return jnp.where(first, jnp.zeros_like(came), came)

    def finish_query(owner):
        lanes = lanes_of(owner)
        mixed, grads, folds = [], [], [[None] * TAPS]
        for half in range(2):
            stored = 1 - flip if half else flip
            conv = back[0, owner, half].astype(F32)
            mixed.append(qkv_ref[0, half, :, lanes].astype(F32) * conv[:ROWS])
            inside = (g_ref[stored, :, lanes].astype(F32) * conv[:ROWS]).astype(BF16).astype(F32)
            beyond = (after_rows(half, 2, lanes) * conv[ROWS:]).astype(BF16).astype(F32)
            source = x_ref[0, stored, :, lanes].astype(F32)
            grads.append(taps_back(0, half, inside, beyond, source, (lanes, folds)))
        for i, (value, grad) in enumerate(zip(in_order(mixed), in_order(grads))):
            mixed_ref[i, :, lanes] = value
            grad_ref[0, i, :, lanes] = grad
        put_part(owner, 0, folds[0])

    def finish_gate(owner):
        lanes = lanes_of(owner)
        grads, folds = [[], [], []], [[None] * TAPS for _ in range(3)]
        for half in range(2):
            stored = 1 - flip if half else flip
            gate_grad = back[1, owner, half].astype(F32)
            sources = {j: x_ref[j, stored, :, lanes].astype(F32) for j in (1, 2)}
            for j in (1, 2):
                other = 3 - j
                ext = jnp.concatenate([sources[other][ROWS - 8 :], after_rows(half, other - 1, lanes)], 0)
                more = w_ref[other, 0:1, lanes] * ext[8:]
                for t in range(1, TAPS):
                    more = more + w_ref[other, t : t + 1, lanes] * ext[8 - t : 16 - t]
                inside = gate_grad[:ROWS] * qkv_ref[other, half, :, lanes].astype(F32)
                beyond = gate_grad[ROWS:] * more.astype(BF16).astype(F32)
                grads[j].append(taps_back(j, half, inside, beyond, sources[j], (lanes, folds)))
        for j in (1, 2):
            for i, grad in enumerate(in_order(grads[j])):
                grad_ref[j, i, :, lanes] = grad
            put_part(owner, j, folds[j])

    def part_back(k):
        owner = ctx_source(me, k)
        return remote(part.at[owner], held.at[me], part_send.at[k], part_recv.at[k], {"ctx": owner})

    own_conv.wait()

    def query_next(i, carry):
        k = turn(i)

        @pl.when(k > 0)
        def _():
            outward(0, k).wait_recv()

        finish_query(ctx_source(me, k))
        return carry

    lax.fori_loop(0, n, query_next, 0)
    to_pair.wait()

    def add_pair(i, carry):
        near[i] = (local[core * half + i] + pair[i]).astype(BF16)
        return carry

    lax.fori_loop(0, half, add_pair, 0)
    across = remote(near, far, dp_send.at[1], dp_recv.at[1], opposite)
    across.start()
    own_grad.wait()

    def start_part(i):
        k = turn(i)

        @pl.when(k > 0)
        def _():
            part_back(k).start()

    def gate_next(i, carry):
        k = turn(i)

        @pl.when(k > 0)
        def _():
            outward(1, k).wait_recv()

        finish_gate(ctx_source(me, k))

        @pl.when(i > 0)
        def _():
            start_part(i - 1)

        return carry

    lax.fori_loop(0, n, gate_next, 0)
    start_part(n - 1)
    held[me] = part[me]
    across.wait()
    lax.fori_loop(0, half, add_far, 0)
    to_whole = remote(filt.at[kept], filt.at[kept], dp_send.at[2], dp_recv.at[2], neighbour)
    to_whole.start()
    for k in STEPS:
        part_back(k).wait_recv()
    dp_held[mine] = jnp.sum(held[...], axis=0)
    sums_out = [
        remote(dp_held.at[mine], dp_held.at[mine], sum_send.at[i], sum_recv.at[i], {"dp": lax.rem(mine + i, 4)})
        for i in range(1, 4)
    ]
    for copy in sums_out:
        copy.start()
    for copy in sums_out:
        copy.wait()
    sums = (dp_held[0] + dp_held[1]) + (dp_held[2] + dp_held[3])
    for j in range(3):
        total[j] = sums[8 * j : 8 * j + TAPS]
    to_whole.wait()
    for copy in halos:
        copy.wait_send()
    for k in STEPS:
        part_back(k).wait_send()
        for a in range(2):
            inward(a, k).wait_send()
            outward(a, k).wait_send()


def hyena(order, long_h, w, x, g):
    outer, outer_t, inner, inner_t, cos_g, sin_g = dft_tables()
    width = x.shape[-1]
    n = width // LANES
    vmem, smem, hbm = (pl.BlockSpec(memory_space=m) for m in (pltpu.VMEM, pltpu.SMEM, pl.ANY))
    cube, sums = (OUTER, LANES, LANES), (24, LANES)
    dma = pltpu.SemaphoreType.DMA
    mixed_shape, grad_shape = (2, ROWS, width), (3, 2, ROWS, width)
    token_blocks, back_blocks = (2, n, 2, ROWS, LANES), (2, n, 2, WIDE, LANES)
    half_cube = (OUTER // 2, LANES, LANES)
    spectrum = (OUTER // 2, 2 * LANES, 2 * LANES)
    stage = (2 * OUTER, LANES, LANES)
    return pl.pallas_call(
        hyena_kernel,
        out_shape=[
            pltpu.VMEM(mixed_shape, BF16),
            pltpu.VMEM(grad_shape, BF16),
            pltpu.VMEM(cube, F32),
            jax.ShapeDtypeStruct((3, TAPS, LANES), F32),
        ],
        in_specs=[smem] * 3 + [vmem] * 6 + [hbm] * 2,
        out_specs=[vmem] * 4,
        scratch_shapes=[
            *[pltpu.VMEM(token_blocks, BF16)] * 2,
            pltpu.VMEM(stage, BF16),
            *[pltpu.VMEM(spectrum, F32)] * 3,
            *[pltpu.VMEM(stage, BF16)] * 2,
            pltpu.VMEM(back_blocks, BF16),
            pltpu.VMEM(cube, F32),
            pltpu.VMEM(half_cube, F32),
            *[pltpu.VMEM(half_cube, BF16)] * 2,
            pltpu.VMEM(back_blocks, BF16),
            *[pltpu.VMEM(grad_shape, BF16)] * 2,
            pltpu.VMEM(mixed_shape, BF16),
            pltpu.VMEM((2, 3, ROWS + 8, LANES), F32),
            *[pltpu.VMEM((n, *sums), F32)] * 2,
            pltpu.VMEM((4, *sums), F32),
            *[pltpu.VMEM((2, 3, 8, width), BF16)] * 4,
            *[dma((2, n))] * 4,
            dma((4,)),
            dma((3,)),
            dma((3,)),
            dma((2,)),
            *[dma((n,))] * 2,
            *[dma((4,))] * 2,
            *[dma((2, 2))] * 2,
        ],
        compiler_params=pltpu.CompilerParams(collective_id=1, has_side_effects=True, vmem_limit_bytes=48 << 20),
        name="hyena",
    )(cos_g, sin_g, order, outer, outer_t, inner, inner_t, long_h, w, x, g)


def on_device(feats, grad_y, short_w, long_h, block_order):
    width = feats.shape[3]
    x = feats.reshape(3, 2, ROWS, width)
    g = grad_y.reshape(2, ROWS, width)
    mixed, grads, filt, short = hyena(block_order, long_h, jnp.transpose(short_w, (1, 0, 2)), x, g)
    return (
        mixed.reshape(grad_y.shape),
        grads.reshape(feats.shape),
        jnp.transpose(short, (1, 0, 2)),
        filt.reshape(OUTER * LANES, LANES),
    )


def solution(mesh):
    placed = (P("dp", None, "ctx", None), P("dp", "ctx", None), P(), P(None, "ctx"), P())
    return jax.shard_map(
        on_device,
        mesh=mesh,
        in_specs=placed,
        out_specs=(P("dp", "ctx", None), P("dp", None, "ctx", None), P(None, None, "ctx"), P(None, "ctx")),
        check_vma=False,
    )
```

```python
import jax
import jax.numpy as jnp
import numpy as np
from jax import lax
from jax.experimental import pallas as pl
from jax.experimental.pallas import tpu as pltpu
from jax.sharding import PartitionSpec as P

MESH = pl.DeviceIdType.MESH
F32 = jnp.float32
BF16 = jnp.bfloat16
LANES = 128
TAPS = 7
ROWS = 64
WIDE = 72
OUTER = 32
GROUPS = 16
ORDER = tuple(range(OUTER // 2)) + tuple(range(OUTER - 1, OUTER // 2 - 1, -1))


def dft_tables():
    k1 = np.arange(OUTER)[:, None, None, None] + 0.5
    r = np.array(ORDER)[None, None, :, None]
    n_out = np.arange(8)[None, :, None, None]
    n_in = np.arange(8)[None, None, None, :]
    angle = 2.0 * np.pi * (r * k1 / 64.0 + n_in * k1 / 8192.0)
    keep = (n_out == n_in).astype(np.float64)
    outer = np.stack([np.cos(angle) * keep, -np.sin(angle) * keep], 1).reshape(OUTER * 16, OUTER * 8)
    n2 = np.arange(LANES)
    turn = 2.0 * np.pi * ((n2[:, None] * n2[None, :]) % LANES) / LANES
    inner = np.block([[np.cos(turn), np.sin(turn)], [-np.sin(turn), np.cos(turn)]])
    group = 2.0 * np.pi * np.arange(GROUPS)[:, None] * 8.0 * (np.arange(OUTER)[None, :] + 0.5) / 8192.0
    half = lambda a: np.asarray(np.asarray(a, np.float32), BF16)
    flat = lambda a: np.asarray(a, np.float32).reshape(-1)
    return (half(outer), half(outer.T / 4096.0), half(inner), half(inner.T), flat(np.cos(group)), flat(np.sin(group)))


def turn(i):
    a, b, c = i % 4, i // 4 % 4, i // 16
    return 8 * ((10 - a - b) % 4) + 4 * ((a + b + c + 1) % 2) + (6 - a) % 4


STEPS = [turn(i) for i in range(32) if turn(i)]


def ctx_peer(me, k):
    y, z, x = me // 8 + k // 8, me // 4 + k // 4, me + k
    return (lax.rem(y, 4) * 2 + lax.rem(z, 2)) * 4 + lax.rem(x, 4)


def ctx_source(me, k):
    y, z, x = me // 8 + 4 - k // 8, me // 4 + k // 4, me + 4 - lax.rem(k, 4)
    return (lax.rem(y, 4) * 2 + lax.rem(z, 2)) * 4 + lax.rem(x, 4)


def remote(src, dst, ssem, rsem, device):
    return pltpu.make_async_remote_copy(
        src_ref=src, dst_ref=dst, send_sem=ssem, recv_sem=rsem, device_id=device, device_id_type=MESH
    )


def wide_rows(h):
    return pl.ds(pl.multiple_of(h * 16, 16), 16)


def place(p):
    return (p, 0) if p < OUTER else (2 * OUTER - 1 - p, 1)


def scalars(cos_ref, sin_ref, h, k):
    first, second = 2 * h * OUTER + k, (2 * h + 1) * OUTER + k
    return cos_ref[first], sin_ref[first], cos_ref[second], sin_ref[second]


def outer_step(cos_ref, sin_ref, outer, pieces, mid, h):
    data = jnp.concatenate(
        [jnp.concatenate([v[:8] for v in pieces], 0), jnp.concatenate([v[8:] for v in pieces], 0)], 1
    ).astype(BF16)
    out = jnp.dot(outer[...], data, preferred_element_type=F32)
    for k in range(OUTER):
        c0, s0, c1, s1 = scalars(cos_ref, sin_ref, h, k)
        re, im = out[16 * k : 16 * k + 8], out[16 * k + 8 : 16 * k + 16]
        re0, re1, im0, im1 = re[:, :LANES], re[:, LANES:], im[:, :LANES], im[:, LANES:]
        mid[2 * k, wide_rows(h), :] = jnp.concatenate([re0 * c0 + im0 * s0, re1 * c1 + im1 * s1], 0).astype(BF16)
        mid[2 * k + 1, wide_rows(h), :] = jnp.concatenate([im0 * c0 - re0 * s0, im1 * c1 - re1 * s1], 0).astype(BF16)


def inner_forward(inner, mid, m):
    rows = [mid[pl.ds(4 * m + 2 * i, 2)].reshape(2 * LANES, LANES) for i in range(2)]
    return jnp.dot(inner[...], jnp.concatenate(rows, 1), preferred_element_type=F32)


def inner_inverse(cos_ref, sin_ref, inner_t, re, im, m, turned):
    prod = jnp.concatenate([re.astype(BF16), im.astype(BF16)], 0)
    back = jnp.dot(inner_t[...], prod, preferred_element_type=F32)
    for i in range(2):
        lanes = slice(i * LANES, (i + 1) * LANES)
        k = 2 * m + i
        for h in range(GROUPS // 2):
            c0, s0, c1, s1 = scalars(cos_ref, sin_ref, h, k)
            re0, re1 = back[16 * h : 16 * h + 8, lanes], back[16 * h + 8 : 16 * h + 16, lanes]
            im0, im1 = (back[LANES + 16 * h + o : LANES + 16 * h + o + 8, lanes] for o in (0, 8))
            rows = slice(16 * h, 16 * h + 16)
            turned[2 * k, rows, :] = jnp.concatenate([re0 * c0 - im0 * s0, re1 * c1 - im1 * s1], 0).astype(BF16)
            turned[2 * k + 1, rows, :] = jnp.concatenate([im0 * c0 + re0 * s0, im1 * c1 + re1 * s1], 0).astype(BF16)


def outer_inverse(outer_t, turned, h):
    values = turned[:, wide_rows(h), :].astype(F32)
    sides = [values[:, o : o + 8].reshape(OUTER * 16, LANES) for o in (0, 8)]
    out = jnp.dot(outer_t[...], jnp.concatenate(sides, 1).astype(BF16), preferred_element_type=F32)
    pieces = []
    for i in range(OUTER):
        part = out[8 * i : 8 * i + 8]
        pieces.append(jnp.concatenate([part[:, :LANES], part[:, LANES:]], 0))
    return pieces


def both_halves(step):
    for odd in range(2):

        def body(i, carry, odd=odd):
            step(4 * odd + i, odd, wide_rows(i))
            return carry

        lax.fori_loop(0, 4, body, 0, unroll=2)


def hyena_kernel(
    cos_ref, sin_ref, order_ref, outer, outer_t, inner, inner_t, long_h, w_ref, x_hbm, g_hbm,
    mixed_ref, grad_ref, filt, total,
    send, recv, mid, spec_h, spec_g, spec_c, turned, cross, out, local, pair, near, far,
    back, qkv_ref, x_ref, g_ref, shifted, part, held, dp_held,
    tail, head, got_tail, got_head,
    send_in, recv_in, send_out, recv_out, own_sem, dp_send, dp_recv,
    load_sem, part_send, part_recv, sum_send, sum_recv, halo_send, halo_recv,
):
    n = send.shape[1]
    me = lax.axis_index("ctx")
    mine = lax.axis_index("dp")
    core = lax.rem(mine, 2)
    neighbour = {"dp": mine + 1 - 2 * core}
    opposite = {"dp": lax.rem(mine + 2, 4)}
    barrier = pltpu.get_barrier_semaphore()
    for k in STEPS:
        pl.semaphore_signal(barrier, inc=1, device_id={"ctx": ctx_peer(me, k)}, device_id_type=MESH)
    diagonal = {"dp": lax.rem(mine + 3 - 2 * core, 4)}
    for device in (neighbour, opposite, diagonal):
        pl.semaphore_signal(barrier, inc=1, device_id=device, device_id_type=MESH)
    loads = [
        pltpu.make_async_copy(source, target, load_sem.at[i])
        for i, (source, target) in enumerate(((x_hbm, x_ref), (g_hbm, g_ref)))
    ]
    for copy in loads:
        copy.start()
    flip = (order_ref[2 * me] != me).astype(jnp.int32)
    for copy in loads:
        copy.wait()
    for way, (ends, starts) in enumerate(((flip, 1 - flip), (1 - flip, flip))):
        for j in range(3):
            tail[way, j] = x_ref[j, ends, ROWS - 8 :, :]
            head[way, j] = x_ref[j + 1, starts, :8, :] if j < 2 else g_ref[starts, :8, :]
    pl.semaphore_wait(barrier, n + 2)
    aside = ({"ctx": lax.rem(me + 1, n)}, {"ctx": lax.rem(me + n - 1, n)})
    halos = [
        remote(source.at[way], target.at[way], halo_send.at[i, way], halo_recv.at[i, way], aside[way])
        for i, (source, target) in enumerate(((tail, got_tail), (head, got_head)))
        for way in range(2)
    ]
    for copy in halos:
        copy.start()

    def inward(a, k):
        peer = ctx_peer(me, k)
        return remote(send.at[a, peer], recv.at[a, me], send_in.at[a, k], recv_in.at[a, k], {"ctx": peer})

    def outward(a, k):
        peer = ctx_peer(me, k)
        return remote(out.at[a, peer], back.at[a, me], send_out.at[a, k], recv_out.at[a, k], {"ctx": peer})

    def filter_outer(h, odd, row):
        del odd, row
        pieces = [long_h[pl.ds(pl.multiple_of(r * LANES + h * 16, 16), 16), :] for r in ORDER]
        outer_step(cos_ref, sin_ref, outer, pieces, mid, h)

    both_halves(filter_outer)

    def filter_inner(m, carry):
        spec_h[m] = inner_forward(inner, mid, m)
        return carry

    lax.fori_loop(0, OUTER // 2, filter_inner, 0, unroll=2)

    for copy in halos[:2]:
        copy.wait_recv()
    first, last = me == 0, me == n - 1

    def lanes_of(owner):
        return pl.ds(pl.multiple_of(owner * LANES, LANES), LANES)

    def featurize(owner):
        lanes = lanes_of(owner)
        for half in range(2):
            stored = 1 - flip if half else flip
            values = []
            for j in range(3):
                came = got_tail[half, j, :, lanes].astype(F32)
                if half == 0:
                    before = jnp.where(first, jnp.zeros_like(came), came)
                else:
                    before = jnp.where(last, tail[0, j, :, lanes].astype(F32), came)
                shifted[half, j, :8] = before
                shifted[half, j, 8:] = x_ref[j, stored, :, lanes].astype(F32)
                acc = None
                for t in range(TAPS):
                    term = w_ref[j, t : t + 1, lanes] * shifted[half, j, pl.ds(8 - t, ROWS), :]
                    acc = term if acc is None else acc + term
                value = acc.astype(BF16)
                qkv_ref[j, half, :, lanes] = value
                values.append(value.astype(F32))
            send[0, owner, half] = (values[1] * values[2]).astype(BF16)
            send[1, owner, half] = (g_ref[stored, :, lanes].astype(F32) * values[0]).astype(BF16)

    def start_gated(i):
        k = turn(i)

        @pl.when(k > 0)
        def _():
            inward(0, k).start()

    featurize(ctx_peer(me, turn(0)))

    def featurize_next(i, carry):
        featurize(ctx_peer(me, turn(i)))
        start_gated(i - 1)
        return carry

    lax.fori_loop(1, n, featurize_next, 0)
    start_gated(n - 1)
    own_in = [pltpu.make_async_copy(send.at[a, me], recv.at[a, me], own_sem.at[a]) for a in range(2)]
    for copy in own_in:
        copy.start()
    for k in STEPS:
        inward(1, k).start()

    def arrive(a):
        own_in[a].wait()
        for k in STEPS:
            inward(a, k).wait_recv()

        def step(h, odd, row):
            places = [place(2 * r + odd) for r in ORDER]
            pieces = [recv[a, owner, half, row, :].astype(F32) for owner, half in places]
            outer_step(cos_ref, sin_ref, outer, pieces, mid, h)

        both_halves(step)

    def depart(a, turned):
        def step(h, odd, row):
            for r, piece in zip(ORDER, outer_inverse(outer_t, turned, h)):
                owner, half = place(2 * r + odd)
                out[a, owner, half, row, :] = piece.astype(BF16)

        both_halves(step)
        for p in range(2 * n):
            owner, half = place(p)
            if p + 1 < 2 * n:
                after, part = place(p + 1)
                out[a, owner, half, ROWS:, :] = out[a, after, part, : WIDE - ROWS, :]
            else:
                out[a, owner, half, ROWS:, :] = jnp.zeros((WIDE - ROWS, LANES), BF16)
        for k in STEPS:
            outward(a, k).start()
        own = pltpu.make_async_copy(out.at[a, me], back.at[a, me], own_sem.at[2 + a])
        own.start()
        return own

    arrive(0)

    def conv_step(m, carry):
        g = inner_forward(inner, mid, m)
        spec_g[m] = g
        h = spec_h[m]
        gr, gi, hr, hi = g[:LANES], g[LANES:], h[:LANES], h[LANES:]
        inner_inverse(cos_ref, sin_ref, inner_t, gr * hr - gi * hi, gr * hi + gi * hr, m, turned)
        return carry

    lax.fori_loop(0, OUTER // 2, conv_step, 0, unroll=2)
    own_conv = depart(0, turned)

    arrive(1)

    def grad_step(m, carry):
        c = inner_forward(inner, mid, m)
        spec_c[m] = c
        h = spec_h[m]
        cr, ci, hr, hi = c[:LANES], c[LANES:], h[:LANES], h[LANES:]
        inner_inverse(cos_ref, sin_ref, inner_t, cr * hr + ci * hi, ci * hr - cr * hi, m, turned)
        return carry

    lax.fori_loop(0, OUTER // 2, grad_step, 0, unroll=2)

    def cross_step(m, carry):
        c, g = spec_c[m], spec_g[m]
        cr, ci, gr, gi = c[:LANES], c[LANES:], g[:LANES], g[LANES:]
        inner_inverse(cos_ref, sin_ref, inner_t, cr * gr + ci * gi, ci * gr - cr * gi, m, cross)
        return carry

    lax.fori_loop(0, OUTER // 2, cross_step, 0, unroll=2)

    def filter_back(h, odd, row):
        del odd, row
        for r, piece in zip(ORDER, outer_inverse(outer_t, cross, h)):
            local[r, wide_rows(h), :] = piece

    both_halves(filter_back)

    half = OUTER // 2
    kept = pl.ds(core * half, half)
    given = pl.ds((1 - core) * half, half)
    to_pair = remote(local.at[given], pair, dp_send.at[0], dp_recv.at[0], neighbour)
    to_pair.start()
    own_grad = depart(1, turned)

    def add_far(i, carry):
        filt[core * half + i] = near[i].astype(F32) + far[i].astype(F32)
        return carry

    for copy in halos[2:]:
        copy.wait_recv()

    def taps_back(j, half, inside, beyond, source, sums):
        shifted[half, j, :ROWS] = inside
        shifted[half, j, ROWS:] = beyond
        acc = None
        for t in range(TAPS):
            value = shifted[half, j, pl.ds(t, ROWS), :]
            term = w_ref[j, t : t + 1, sums[0]] * value
            acc = term if acc is None else acc + term
            fold = jnp.sum((source * value).reshape(8, 8, LANES), axis=0)
            sums[1][j][t] = fold if half == 0 else sums[1][j][t] + fold
        return acc

    def put_part(owner, j, folds):
        rows = [jnp.sum(value, axis=0, keepdims=True) for value in folds]
        part[owner, 8 * j : 8 * j + 8, :] = jnp.concatenate([*rows, jnp.zeros((1, LANES), F32)], 0)

    def in_order(values):
        keep = flip == 0
        return [jnp.where(keep, values[i], values[1 - i]).astype(BF16) for i in range(2)]

    def after_rows(half, rim, lanes):
        came = got_head[1 - half, rim, :, lanes].astype(F32)
        if half == 0:
            return jnp.where(last, head[0, rim, :, lanes].astype(F32), came)
        return jnp.where(first, jnp.zeros_like(came), came)

    def finish_query(owner):
        lanes = lanes_of(owner)
        mixed, grads, folds = [], [], [[None] * TAPS]
        for half in range(2):
            stored = 1 - flip if half else flip
            conv = back[0, owner, half].astype(F32)
            mixed.append(qkv_ref[0, half, :, lanes].astype(F32) * conv[:ROWS])
            inside = (g_ref[stored, :, lanes].astype(F32) * conv[:ROWS]).astype(BF16).astype(F32)
            beyond = (after_rows(half, 2, lanes) * conv[ROWS:]).astype(BF16).astype(F32)
            source = x_ref[0, stored, :, lanes].astype(F32)
            grads.append(taps_back(0, half, inside, beyond, source, (lanes, folds)))
        for i, (value, grad) in enumerate(zip(in_order(mixed), in_order(grads))):
            mixed_ref[i, :, lanes] = value
            grad_ref[0, i, :, lanes] = grad
        put_part(owner, 0, folds[0])

    def finish_gate(owner):
        lanes = lanes_of(owner)
        grads, folds = [[], [], []], [[None] * TAPS for _ in range(3)]
        for half in range(2):
            stored = 1 - flip if half else flip
            gate_grad = back[1, owner, half].astype(F32)
            sources = {j: x_ref[j, stored, :, lanes].astype(F32) for j in (1, 2)}
            for j in (1, 2):
                other = 3 - j
                ext = jnp.concatenate([sources[other][ROWS - 8 :], after_rows(half, other - 1, lanes)], 0)
                more = w_ref[other, 0:1, lanes] * ext[8:]
                for t in range(1, TAPS):
                    more = more + w_ref[other, t : t + 1, lanes] * ext[8 - t : 16 - t]
                inside = gate_grad[:ROWS] * qkv_ref[other, half, :, lanes].astype(F32)
                beyond = gate_grad[ROWS:] * more.astype(BF16).astype(F32)
                grads[j].append(taps_back(j, half, inside, beyond, sources[j], (lanes, folds)))
        for j in (1, 2):
            for i, grad in enumerate(in_order(grads[j])):
                grad_ref[j, i, :, lanes] = grad
            put_part(owner, j, folds[j])

    def part_back(k):
        owner = ctx_source(me, k)
        return remote(part.at[owner], held.at[me], part_send.at[k], part_recv.at[k], {"ctx": owner})

    own_conv.wait()

    def query_next(i, carry):
        k = turn(i)

        @pl.when(k > 0)
        def _():
            outward(0, k).wait_recv()

        finish_query(ctx_source(me, k))
        return carry

    lax.fori_loop(0, n, query_next, 0)
    to_pair.wait()

    def add_pair(i, carry):
        near[i] = (local[core * half + i] + pair[i]).astype(BF16)
        return carry

    lax.fori_loop(0, half, add_pair, 0)
    across = remote(near, far, dp_send.at[1], dp_recv.at[1], opposite)
    across.start()
    own_grad.wait()

    def start_part(i):
        k = turn(i)

        @pl.when(k > 0)
        def _():
            part_back(k).start()

    def gate_next(i, carry):
        k = turn(i)

        @pl.when(k > 0)
        def _():
            outward(1, k).wait_recv()

        finish_gate(ctx_source(me, k))

        @pl.when(i > 0)
        def _():
            start_part(i - 1)

        return carry

    lax.fori_loop(0, n, gate_next, 0)
    start_part(n - 1)
    held[me] = part[me]
    for k in STEPS:
        part_back(k).wait_recv()
    dp_held[mine] = jnp.sum(held[...], axis=0)
    sums_out = [
        remote(dp_held.at[mine], dp_held.at[mine], sum_send.at[i], sum_recv.at[i], {"dp": lax.rem(mine + i, 4)})
        for i in range(1, 4)
    ]
    for copy in sums_out:
        copy.start()
    across.wait()
    lax.fori_loop(0, half, add_far, 0)
    to_whole = remote(filt.at[kept], filt.at[kept], dp_send.at[2], dp_recv.at[2], neighbour)
    to_whole.start()
    for copy in sums_out:
        copy.wait()
    sums = (dp_held[0] + dp_held[1]) + (dp_held[2] + dp_held[3])
    for j in range(3):
        total[j] = sums[8 * j : 8 * j + TAPS]
    to_whole.wait()
    for copy in halos:
        copy.wait_send()
    for k in STEPS:
        part_back(k).wait_send()
        for a in range(2):
            inward(a, k).wait_send()
            outward(a, k).wait_send()


def hyena(order, long_h, w, x, g):
    outer, outer_t, inner, inner_t, cos_g, sin_g = dft_tables()
    width = x.shape[-1]
    n = width // LANES
    vmem, smem, hbm = (pl.BlockSpec(memory_space=m) for m in (pltpu.VMEM, pltpu.SMEM, pl.ANY))
    cube, sums = (OUTER, LANES, LANES), (24, LANES)
    dma = pltpu.SemaphoreType.DMA
    mixed_shape, grad_shape = (2, ROWS, width), (3, 2, ROWS, width)
    token_blocks, back_blocks = (2, n, 2, ROWS, LANES), (2, n, 2, WIDE, LANES)
    half_cube = (OUTER // 2, LANES, LANES)
    spectrum = (OUTER // 2, 2 * LANES, 2 * LANES)
    stage = (2 * OUTER, LANES, LANES)
    return pl.pallas_call(
        hyena_kernel,
        out_shape=[
            pltpu.VMEM(mixed_shape, BF16),
            pltpu.VMEM(grad_shape, BF16),
            pltpu.VMEM(cube, F32),
            jax.ShapeDtypeStruct((3, TAPS, LANES), F32),
        ],
        in_specs=[smem] * 3 + [vmem] * 6 + [hbm] * 2,
        out_specs=[vmem] * 4,
        scratch_shapes=[
            *[pltpu.VMEM(token_blocks, BF16)] * 2,
            pltpu.VMEM(stage, BF16),
            *[pltpu.VMEM(spectrum, F32)] * 3,
            *[pltpu.VMEM(stage, BF16)] * 2,
            pltpu.VMEM(back_blocks, BF16),
            pltpu.VMEM(cube, F32),
            pltpu.VMEM(half_cube, F32),
            *[pltpu.VMEM(half_cube, BF16)] * 2,
            pltpu.VMEM(back_blocks, BF16),
            *[pltpu.VMEM(grad_shape, BF16)] * 2,
            pltpu.VMEM(mixed_shape, BF16),
            pltpu.VMEM((2, 3, ROWS + 8, LANES), F32),
            *[pltpu.VMEM((n, *sums), F32)] * 2,
            pltpu.VMEM((4, *sums), F32),
            *[pltpu.VMEM((2, 3, 8, width), BF16)] * 4,
            *[dma((2, n))] * 4,
            dma((4,)),
            dma((3,)),
            dma((3,)),
            dma((2,)),
            *[dma((n,))] * 2,
            *[dma((4,))] * 2,
            *[dma((2, 2))] * 2,
        ],
        compiler_params=pltpu.CompilerParams(collective_id=1, has_side_effects=True, vmem_limit_bytes=48 << 20),
        name="hyena",
    )(cos_g, sin_g, order, outer, outer_t, inner, inner_t, long_h, w, x, g)


def on_device(feats, grad_y, short_w, long_h, block_order):
    width = feats.shape[3]
    x = feats.reshape(3, 2, ROWS, width)
    g = grad_y.reshape(2, ROWS, width)
    mixed, grads, filt, short = hyena(block_order, long_h, jnp.transpose(short_w, (1, 0, 2)), x, g)
    return (
        mixed.reshape(grad_y.shape),
        grads.reshape(feats.shape),
        jnp.transpose(short, (1, 0, 2)),
        filt.reshape(OUTER * LANES, LANES),
    )


def solution(mesh):
    placed = (P("dp", None, "ctx", None), P("dp", "ctx", None), P(), P(None, "ctx"), P())
    return jax.shard_map(
        on_device,
        mesh=mesh,
        in_specs=placed,
        out_specs=(P("dp", "ctx", None), P("dp", None, "ctx", None), P(None, None, "ctx"), P(None, "ctx")),
        check_vma=False,
    )
```
